32 devices in a mesh: dom: 32 (over z, y, x, core).
Axes of the slice: x: 2, y: 2, z: 4, core: 2. Of those that a mesh axis runs over, the one named last changes fastest.
Arguments:
- features: bfloat16 [65536, 256], P('dom'), may hold values from -6 to 6
- self_weight: bfloat16 [256, 256], replicated, may hold values from -0.375 to 0.375
- neighbour_weight: bfloat16 [256, 256], replicated, may hold values from -0.375 to 0.375
- send_lists: int32 [32, 32, 8], P('dom'), may hold values from 0 to 2047
- hub_nodes: int32 [32, 8], P('dom'), may hold values from 0 to 2047
- neighbours: int32 [65536, 16], P('dom'), may hold values from 0 to 2559
- counts: int32 [65536], P('dom'), may hold values from 1 to 16
- cotangent: bfloat16 [65536, 256], P('dom'), may hold values from -6 to 6
Outputs:
- activations: bfloat16 [65536, 256], P('dom')
- grad_features: float32 [65536, 256], P('dom')
- grad_weights: float32 [512, 256], P('dom')
The draws below stay inside these ranges and needn't reach their ends.
All inputs are finite; a program needn't handle non-finite values.
Results may differ from the reference program's by a relative error of at most 0.0032.
Values may be sent and summed in bfloat16 or wider, within the bound.
A program may use at most 64 MiB of HBM per device.

```python
import jax
import jax.numpy as jnp
from jax import lax

F = 256
H = 256
FAN = 16
NODE_DEV = 2048
BND = 8
HUB_DEV = 8
NODES = 65536
TABLE = 2560
N_DOM = 32


def place_ends(drawn, stream_key, least, largest):
    index_at = [jax.random.randint(jax.random.fold_in(stream_key, axis), (), 0, length) for axis, length in enumerate(drawn.shape)]
    longest = drawn.shape.index(max(drawn.shape))
    beside = index_at[:longest] + [(index_at[longest] + 1) % drawn.shape[longest]] + index_at[longest + 1:]
    return drawn.at[tuple(index_at)].set(least).at[tuple(beside)].set(largest)


def raised(result, rng, source, target, parts, factor):
    owner, partner = [(jnp.arange(result.shape[dim]) // (result.shape[dim] // parts)).reshape([-1 if axis == dim else 1 for axis in range(result.ndim)]) for dim in (source, target)]
    chosen = jax.random.permutation(rng, parts)[partner]
    strong = (owner == chosen) | (owner == (partner + parts // 2) % parts)
    return jnp.where(strong, factor * result, result)


def block_levels(own_key, shape, shards, least, high):
    level, own = 1.0, jax.random.fold_in(own_key, 6)
    for position, blocks in shards:
        draws = jnp.exp(jax.random.uniform(jax.random.fold_in(own, position), (blocks,), jnp.float32, least / len(shards), high / len(shards)))
        level = level * jnp.repeat(draws, shape[position] // blocks).reshape([-1 if axis == position else 1 for axis in range(len(shape))])
    return level


def bell_draw(stream_key, shape, spread, limit, pieces=(), kind=jnp.bfloat16):
    array = jax.random.normal(stream_key, shape, jnp.float32) * spread
    if len(pieces) > 0:
        array = block_levels(stream_key, shape, pieces, -0.22, 0.18) * array
    return jnp.clip(array, min=-limit, max=limit).astype(kind)


def noise_with(key, extent, width, limit, shards, heavy, held_as=jnp.bfloat16):
    result = width * jax.random.normal(key, extent, jnp.float32)
    if shards:
        result = result * block_levels(key, extent, shards, -0.22, 0.18)
    return jnp.clip(raised(result, jax.random.fold_in(key, 3), *heavy), -limit, limit).astype(held_as)


def setup_inputs(seed: int = 0) -> dict:
    splits = jax.random.split(jax.random.key(seed), 9)
    features = noise_with(splits[0], (NODES, F), 1.0, 6.0, ((0, 32),), (0, 1, 32, 2.75))
    self_weight = bell_draw(splits[1], (F, H), F ** -0.5, 0.375)
    neighbour_weight = bell_draw(splits[2], (F, H), F ** -0.5, 0.375)
    send_lists = place_ends(jax.random.randint(splits[3], (N_DOM, N_DOM, BND), 0, NODE_DEV), jax.random.fold_in(splits[3], 1), 0, NODE_DEV - 1).astype(jnp.int32)
    hub_nodes = place_ends(jax.random.randint(splits[4], (N_DOM, HUB_DEV), 0, NODE_DEV), jax.random.fold_in(splits[4], 1), 0, NODE_DEV - 1).astype(jnp.int32)
    neighbours = place_ends(jax.random.randint(splits[5], (NODES, FAN), 0, TABLE), jax.random.fold_in(splits[5], 1), 0, TABLE - 1).astype(jnp.int32)
    counts = place_ends(jax.random.randint(splits[6], (NODES,), 1, FAN + 1), jax.random.fold_in(splits[6], 1), 1, FAN).astype(jnp.int32)
    cotangent = bell_draw(splits[7], (NODES, H), 1.0, 6.0, ((0, 32),))
    return dict(features=features, self_weight=self_weight, neighbour_weight=neighbour_weight, send_lists=send_lists, hub_nodes=hub_nodes, neighbours=neighbours, counts=counts, cotangent=cotangent)


def resolve(send_lists, hub_nodes, neighbours):
    partition = (jnp.arange(NODES, dtype=jnp.int32) // NODE_DEV)[:, None]
    table_slot = neighbours
    bound_slot = table_slot - NODE_DEV
    bound_peer = jnp.clip(bound_slot // BND, 0, N_DOM - 1)
    bound_pos = bound_slot % BND
    flat_lists = send_lists.reshape(-1)
    bound_index = (bound_peer * (N_DOM * BND) + partition * BND + bound_pos).astype(jnp.int32)
    bound_source = bound_peer * NODE_DEV + jnp.take(flat_lists, bound_index)
    hub_slot = table_slot - NODE_DEV - N_DOM * BND
    hub_owner = jnp.clip(hub_slot // HUB_DEV, 0, N_DOM - 1)
    hub_index = (hub_owner * HUB_DEV + hub_slot % HUB_DEV).astype(jnp.int32)
    hub_source = hub_owner * NODE_DEV + jnp.take(hub_nodes.reshape(-1), hub_index)
    local_source = partition * NODE_DEV + table_slot
    source = jnp.where(table_slot < NODE_DEV, local_source,
                       jnp.where(table_slot < NODE_DEV + N_DOM * BND, bound_source, hub_source))
    return source.astype(jnp.int32)


def reference(features, self_weight, neighbour_weight, send_lists, hub_nodes, neighbours, counts, cotangent):
    source = resolve(send_lists, hub_nodes, neighbours)
    usable = jnp.arange(FAN, dtype=jnp.int32)[None, :] < counts[:, None]
    degree = counts.astype(jnp.float32)[:, None]
    blocked_source = source.reshape(N_DOM, NODE_DEV, FAN)
    blocked_usable = usable.reshape(N_DOM, NODE_DEV, FAN)
    blocked_degree = degree.reshape(N_DOM, NODE_DEV, 1)

    def mean_block(block_args):
        block_source, block_usable, block_degree = block_args
        gathered = jnp.take(features, block_source, axis=0).astype(jnp.float32)
        summed = jnp.sum(jnp.where(block_usable[:, :, None], gathered, 0.0), axis=1)
        return (summed / block_degree).astype(jnp.bfloat16)

    mean = lax.map(mean_block, (blocked_source, blocked_usable, blocked_degree)).reshape(NODES, F)
    pre = jnp.dot(features, self_weight, preferred_element_type=jnp.float32) + jnp.dot(mean, neighbour_weight, preferred_element_type=jnp.float32)
    sigmoid_pre = jax.nn.sigmoid(pre)
    activations = (pre * sigmoid_pre).astype(jnp.bfloat16)
    grad_pre = (cotangent.astype(jnp.float32) * sigmoid_pre * (1.0 + pre * (1.0 - sigmoid_pre))).astype(jnp.bfloat16)
    grad_mean = jnp.dot(grad_pre, neighbour_weight.T, preferred_element_type=jnp.float32)
    grad_self = jnp.dot(grad_pre, self_weight.T, preferred_element_type=jnp.float32)
    edge_weight = (grad_mean / degree).reshape(N_DOM, NODE_DEV, F)

    def add_block(grad_total, block_args):
        block_source, block_usable, block_weight = block_args
        contrib = jnp.where(block_usable[:, :, None], block_weight[:, None, :], 0.0).reshape(-1, F)
        return grad_total.at[block_source.reshape(-1)].add(contrib), None

    grad_features, unused = lax.scan(add_block, grad_self, (blocked_source, blocked_usable, edge_weight))
    dims = (((0,), (0,)), ((), ()))
    upper = lax.dot_general(features, grad_pre, dims, preferred_element_type=jnp.float32)
    lower = lax.dot_general(mean, grad_pre, dims, preferred_element_type=jnp.float32)
    grad_weights = jnp.concatenate([upper, lower], axis=0)
    return activations, grad_features, grad_weights
```

```python
import functools

import jax
import jax.numpy as jnp
from jax import lax
from jax.experimental import pallas as pl
from jax.experimental.pallas import tpu as pltpu
from jax.sharding import PartitionSpec as P

LO = 256
BLOCK = 256
BF16 = jnp.bfloat16
F32 = jnp.float32
PARAMS = pltpu.CompilerParams(vmem_limit_bytes=56 * 1024 * 1024)


def dot(a, b, ca, cb):
    return lax.dot_general(a, b, (((ca,), (cb,)), ((), ())), preferred_element_type=F32)


def one_hot_rows(list_column, width):
    lanes = lax.broadcasted_iota(jnp.int32, (list_column.shape[0], width), 1)
    return jnp.where(list_column == lanes, 1.0, 0.0).astype(BF16)


def pack_kernel(lists_ref, features_ref, packed_ref):
    picks = one_hot_rows(lists_ref[...], features_ref.shape[0])
    packed_ref[...] = dot(picks, features_ref[...], 1, 0).astype(BF16)


def count_kernel(local_blocks, index_ref, features_ref, count_ref, summed_ref):
    blocks = count_ref.shape[0]
    groups, lanes = index_ref.shape
    fan = lanes // 16
    rows16 = lax.broadcasted_iota(jnp.int32, (16, lanes), 0)
    cols16 = lax.broadcasted_iota(jnp.int32, (16, lanes), 1) // fan
    own = rows16 == cols16
    low_ids = lax.broadcasted_iota(jnp.int32, (LO, lanes), 0).astype(F32).astype(BF16)
    one = jnp.ones((), BF16)
    zero = jnp.zeros((), BF16)
    for group in range(groups):
        row = index_ref[group : group + 1, :]
        high = jnp.where(own, jnp.broadcast_to(row >> 8, (16, lanes)), -1)
        high = high.astype(F32).astype(BF16)
        low = jnp.broadcast_to((row & (LO - 1)).astype(F32), (16, lanes)).astype(BF16)
        low = jnp.concatenate([low] * (LO // 16), axis=0)
        low_hot = jnp.where(low_ids == low, one, zero)
        high_hot = jnp.concatenate(
            [jnp.where(high == jnp.full((), h, BF16), one, zero) for h in range(blocks)], axis=0
        )
        counted = dot(high_hot, low_hot, 1, 1).astype(BF16)
        for h in range(blocks):
            count_ref[h, 16 * group : 16 * group + 16, :] = counted[16 * h : 16 * h + 16]
    total = jnp.zeros(summed_ref.shape, F32)
    for h in range(local_blocks):
        total = total + dot(count_ref[h], features_ref[h * LO : (h + 1) * LO, :], 1, 0)
    summed_ref[...] = total


def node_kernel(
    summed_ref, count_ref, table_ref, features_ref, cotangent_ref, degree_column_ref,
    degree_row_ref, self_ref, neighbour_ref,
    activations_ref, edge_ref, self_grad_ref, send_ref, weight_ref, send_acc, weight_acc,
):
    step = pl.program_id(0)
    width = features_ref.shape[1]
    remote_blocks = count_ref.shape[0]

    @pl.when(step == 0)
    def _():
        send_acc[...] = jnp.zeros_like(send_acc)
        weight_acc[...] = jnp.zeros_like(weight_acc)

    total = summed_ref[...]
    for h in range(remote_blocks):
        total = total + dot(count_ref[h], table_ref[h * LO : (h + 1) * LO, :], 1, 0)
    mean = (total / degree_column_ref[...]).astype(BF16)
    features = features_ref[...]
    pre = dot(features, self_ref[...], 1, 0) + dot(mean, neighbour_ref[...], 1, 0)
    sig = jax.nn.sigmoid(pre)
    activations_ref[...] = (pre * sig).astype(BF16)
    grad_pre = (cotangent_ref[...].astype(F32) * sig * (1.0 + pre * (1.0 - sig))).astype(BF16)
    edge = (dot(neighbour_ref[...], grad_pre, 1, 1) / degree_row_ref[...]).astype(BF16)
    edge_ref[...] = edge
    self_grad_ref[...] = dot(self_ref[...], grad_pre, 1, 1)
    for h in range(remote_blocks):
        send_acc[:, h * LO : (h + 1) * LO] += dot(edge, count_ref[h], 1, 0)
    weight_acc[:width, :] += dot(features, grad_pre, 0, 0)
    weight_acc[width:, :] += dot(mean, grad_pre, 0, 0)

    @pl.when(step == pl.num_programs(0) - 1)
    def _():
        send_ref[...] = send_acc[...].T.astype(BF16)
        weight_ref[...] = weight_acc[...].astype(BF16)


def local_kernel(count_ref, edge_ref, self_grad_ref, out_ref):
    out_ref[...] = self_grad_ref[...] + dot(edge_ref[...], count_ref[0], 1, 0)


def final_kernel(part_ref, lists_ref, returned_ref, out_ref):
    nodes = out_ref.shape[0]
    lanes = lax.broadcasted_iota(jnp.int32, (lists_ref.shape[0], nodes), 1)
    lanes = lanes + pl.program_id(0) * nodes
    picks = jnp.where(lists_ref[...] == lanes, 1.0, 0.0).astype(BF16)
    out_ref[...] = (part_ref[...] + dot(returned_ref[...], picks, 0, 0)).T


def body(
    features, self_weight, neighbour_weight, send_lists, hub_nodes, neighbours, counts, cotangent
):
    nodes, width = features.shape
    fan = neighbours.shape[1]
    peers = lax.axis_size("dom")
    per_peer = send_lists.shape[2]
    hubs = hub_nodes.shape[1]
    both = per_peer + hubs
    remote = peers * both
    local_blocks = nodes // LO
    blocks = local_blocks + remote // LO
    remote_blocks = blocks - local_blocks
    steps = nodes // BLOCK

    lists = jnp.concatenate(
        [send_lists[0], jnp.broadcast_to(hub_nodes, (peers, hubs))], axis=1
    ).reshape(remote, 1)
    packed = pl.pallas_call(
        pack_kernel,
        out_shape=jax.ShapeDtypeStruct((remote, width), BF16),
        compiler_params=PARAMS,
        name="pack",
    )(lists, features)
    arrived = lax.all_to_all(
        packed.reshape(peers, both, width), "dom", split_axis=0, concat_axis=0, tiled=True
    ).reshape(remote, width)

    past = neighbours - nodes
    hub_past = past - peers * per_peer
    remapped = jnp.where(
        past < 0,
        neighbours,
        nodes
        + jnp.where(
            hub_past < 0,
            (past // per_peer) * both + past % per_peer,
            (hub_past // hubs) * both + per_peer + hub_past % hubs,
        ),
    )
    usable = jnp.arange(fan, dtype=jnp.int32)[None, :] < counts[:, None]
    index = jnp.where(usable, remapped, -1).reshape(nodes // 16, 16 * fan)

    count, summed = pl.pallas_call(
        functools.partial(count_kernel, local_blocks),
        grid=(steps,),
        in_specs=[
            pl.BlockSpec((BLOCK // 16, 16 * fan), lambda i: (i, 0)),
            pl.BlockSpec((nodes, width), lambda i: (0, 0)),
        ],
        out_specs=[
            pl.BlockSpec((blocks, BLOCK, LO), lambda i: (0, i, 0)),
            pl.BlockSpec((BLOCK, width), lambda i: (i, 0)),
        ],
        out_shape=[
            jax.ShapeDtypeStruct((blocks, nodes, LO), BF16),
            jax.ShapeDtypeStruct((nodes, width), F32),
        ],
        compiler_params=PARAMS,
        cost_estimate=pl.CostEstimate(
            flops=4 * nodes * blocks * LO * width, bytes_accessed=16 << 20, transcendentals=0
        ),
        name="count",
    )(index, features)

    degree = counts.astype(F32)
    whole = lambda i: (0, 0)
    activations, edge, self_grad, send, weight = pl.pallas_call(
        node_kernel,
        grid=(steps,),
        in_specs=[
            pl.BlockSpec((BLOCK, width), lambda i: (i, 0)),
            pl.BlockSpec(
                (remote_blocks, BLOCK, LO), lambda i: (local_blocks // remote_blocks, i, 0)
            ),
            pl.BlockSpec((remote, width), whole),
            pl.BlockSpec((BLOCK, width), lambda i: (i, 0)),
            pl.BlockSpec((BLOCK, width), lambda i: (i, 0)),
            pl.BlockSpec((BLOCK, 1), lambda i: (i, 0)),
            pl.BlockSpec((1, BLOCK), lambda i: (0, i)),
            pl.BlockSpec((width, width), whole),
            pl.BlockSpec((width, width), whole),
        ],
        out_specs=[
            pl.BlockSpec((BLOCK, width), lambda i: (i, 0)),
            pl.BlockSpec((width, BLOCK), lambda i: (0, i)),
            pl.BlockSpec((width, BLOCK), lambda i: (0, i)),
            pl.BlockSpec((remote, width), whole),
            pl.BlockSpec((2 * width, width), whole),
        ],
        out_shape=[
            jax.ShapeDtypeStruct((nodes, width), BF16),
            jax.ShapeDtypeStruct((width, nodes), BF16),
            jax.ShapeDtypeStruct((width, nodes), F32),
            jax.ShapeDtypeStruct((remote, width), BF16),
            jax.ShapeDtypeStruct((2 * width, width), BF16),
        ],
        scratch_shapes=[
            pltpu.VMEM((width, remote), F32),
            pltpu.VMEM((2 * width, width), F32),
        ],
        compiler_params=PARAMS,
        name="node",
    )(
        summed, count, arrived, features, cotangent, degree[:, None], degree[None, :],
        self_weight, neighbour_weight,
    )
    outgoing = jnp.concatenate(
        [send.reshape(peers, both, width), weight.reshape(peers, 2 * width // peers, width)],
        axis=1,
    )
    returned = lax.all_to_all(outgoing, "dom", split_axis=0, concat_axis=0, tiled=True)

    part = pl.pallas_call(
        local_kernel,
        grid=(local_blocks,),
        in_specs=[
            pl.BlockSpec((1, nodes, LO), lambda h: (h, 0, 0)),
            pl.BlockSpec((width, nodes), whole),
            pl.BlockSpec((width, LO), lambda h: (0, h)),
        ],
        out_specs=pl.BlockSpec((width, LO), lambda h: (0, h)),
        out_shape=jax.ShapeDtypeStruct((width, nodes), F32),
        compiler_params=PARAMS,
        cost_estimate=pl.CostEstimate(
            flops=2 * nodes * nodes * width, bytes_accessed=12 << 20, transcendentals=0
        ),
        name="local",
    )(count, edge, self_grad)

    grad_features = pl.pallas_call(
        final_kernel,
        grid=(nodes // 512,),
        in_specs=[
            pl.BlockSpec((width, 512), lambda i: (0, i)),
            pl.BlockSpec((remote, 1), whole),
            pl.BlockSpec((remote, width), whole),
        ],
        out_specs=pl.BlockSpec((512, width), lambda i: (i, 0)),
        out_shape=jax.ShapeDtypeStruct((nodes, width), F32),
        compiler_params=PARAMS,
        name="final",
    )(part, lists, returned[:, :both].reshape(remote, width))
    grad_weights = jnp.sum(returned[:, both:].astype(F32), axis=0)
    return (activations, grad_features, grad_weights)


def solution(mesh):
    in_specs = (
        P("dom", None),
        P(),
        P(),
        P("dom", None, None),
        P("dom", None),
        P("dom", None),
        P("dom"),
        P("dom", None),
    )
    out_specs = (P("dom", None), P("dom", None), P("dom", None))
    return jax.shard_map(body, mesh=mesh, in_specs=in_specs, out_specs=out_specs, check_vma=False)
```

```python
import functools

import jax
import jax.numpy as jnp
from jax import lax
from jax.experimental import pallas as pl
from jax.experimental.pallas import tpu as pltpu
from jax.sharding import PartitionSpec as P

LO = 256
BLOCK = 256
BF16 = jnp.bfloat16
F32 = jnp.float32
MESH = pl.DeviceIdType.MESH


def dot(a, b, ca, cb):
    return lax.dot_general(a, b, (((ca,), (cb,)), ((), ())), preferred_element_type=F32)


def whole_kernel(
    peers,
    index_ref, lists_ref, degree_column_ref, degree_row_ref, features_ref, cotangent_ref,
    self_ref, neighbour_ref,
    activations_ref, out_ref, weight_out_ref,
    packed, table, count, summed, edge, part, mean_all, pre_grad, send, returned,
    weight_acc, weight_send, weight_in,
    send_sem, recv_sem, back_send_sem, back_recv_sem, weight_send_sem, weight_recv_sem,
):
    me = lax.axis_index("dom")
    nodes, width = features_ref.shape
    remote = packed.shape[0]
    both = remote // peers
    blocks = count.shape[0]
    local_blocks = nodes // LO
    remote_blocks = blocks - local_blocks
    lanes = index_ref.shape[1]
    fan = lanes // 16
    share = weight_send.shape[1]
    own = pl.ds(pl.multiple_of(me * both, both), both)

    barrier = pltpu.get_barrier_semaphore()

    @pl.loop(1, peers)
    def _(p):
        pl.semaphore_signal(
            barrier, inc=1, device_id=(lax.rem(me + p, peers),), device_id_type=MESH
        )

    for start in range(0, remote, 512):
        rows = lists_ref[start : start + 512, :]
        ids = lax.broadcasted_iota(jnp.int32, (512, nodes), 1)
        picks = jnp.where(rows == ids, 1.0, 0.0).astype(BF16)
        packed[start : start + 512, :] = dot(picks, features_ref[...], 1, 0).astype(BF16)
    table[own, :] = packed[own, :]
    pl.semaphore_wait(barrier, peers - 1)

    @pl.loop(1, peers)
    def _(p):
        peer = lax.rem(me + p, peers)
        pltpu.make_async_remote_copy(
            src_ref=packed.at[pl.ds(pl.multiple_of(peer * both, both), both)],
            dst_ref=table.at[own],
            send_sem=send_sem,
            recv_sem=recv_sem,
            device_id=(peer,),
            device_id_type=MESH,
        ).start()

    rows16 = lax.broadcasted_iota(jnp.int32, (16, lanes), 0)
    cols16 = lax.broadcasted_iota(jnp.int32, (16, lanes), 1) // fan
    mine = rows16 == cols16
    low_ids = lax.broadcasted_iota(jnp.int32, (LO, lanes), 0).astype(F32).astype(BF16)
    one = jnp.ones((), BF16)
    zero = jnp.zeros((), BF16)

    @pl.loop(0, nodes // BLOCK)
    def _(step):
        groups = BLOCK // 16
        index = index_ref[pl.ds(pl.multiple_of(step * groups, groups), groups), :]
        for group in range(groups):
            row = index[group : group + 1, :]
            high = jnp.where(mine, jnp.broadcast_to(row >> 8, (16, lanes)), -1)
            high = high.astype(F32).astype(BF16)
            low = jnp.broadcast_to((row & (LO - 1)).astype(F32), (16, lanes)).astype(BF16)
            low = jnp.concatenate([low] * (LO // 16), axis=0)
            low_hot = jnp.where(low_ids == low, one, zero)
            high_hot = jnp.concatenate(
                [jnp.where(high == jnp.full((), h, BF16), one, zero) for h in range(blocks)],
                axis=0,
            )
            counted = dot(high_hot, low_hot, 1, 1).astype(BF16)
            at = pl.ds(pl.multiple_of(step * BLOCK + 16 * group, 16), 16)
            for h in range(blocks):
                count[h, at, :] = counted[16 * h : 16 * h + 16]
        at = pl.ds(pl.multiple_of(step * BLOCK, BLOCK), BLOCK)
        total = jnp.zeros((BLOCK, width), F32)
        for h in range(local_blocks):
            total = total + dot(count[h, at, :], features_ref[h * LO : (h + 1) * LO, :], 1, 0)
        summed[at, :] = total

    others = pl.ds(0, (peers - 1) * both)
    pltpu.make_async_copy(table.at[others], table.at[others], recv_sem).wait()

    @pl.loop(0, nodes // BLOCK)
    def _(step):
        at = pl.ds(pl.multiple_of(step * BLOCK, BLOCK), BLOCK)
        total = summed[at, :]
        for h in range(remote_blocks):
            total = total + dot(
                count[local_blocks + h, at, :], table[h * LO : (h + 1) * LO, :], 1, 0
            )
        mean = (total / degree_column_ref[at, :]).astype(BF16)
        mean_all[at, :] = mean
        pre = dot(features_ref[at, :], self_ref[...], 1, 0) + dot(mean, neighbour_ref[...], 1, 0)
        sig = jax.nn.sigmoid(pre)
        activations_ref[at, :] = (pre * sig).astype(BF16)
        grad_pre = (
            cotangent_ref[at, :].astype(F32) * sig * (1.0 + pre * (1.0 - sig))
        ).astype(BF16)
        pre_grad[at, :] = grad_pre
        edge[:, at] = (dot(neighbour_ref[...], grad_pre, 1, 1) / degree_row_ref[:, at]).astype(BF16)
        part[:, at] = dot(self_ref[...], grad_pre, 1, 1)

    for h in range(remote_blocks):
        send[h * LO : (h + 1) * LO, :] = dot(edge[...], count[local_blocks + h], 1, 0).T.astype(BF16)
    returned[own, :] = send[own, :]

    @pl.loop(1, peers)
    def _(p):
        peer = lax.rem(me + p, peers)
        pltpu.make_async_remote_copy(
            src_ref=send.at[pl.ds(pl.multiple_of(peer * both, both), both)],
            dst_ref=returned.at[own],
            send_sem=back_send_sem,
            recv_sem=back_recv_sem,
            device_id=(peer,),
            device_id_type=MESH,
        ).start()

    weight_acc[:width, :] = dot(features_ref[...], pre_grad[...], 0, 0)
    weight_acc[width:, :] = dot(mean_all[...], pre_grad[...], 0, 0)
    for p in range(peers):
        weight_send[p] = weight_acc[p * share : (p + 1) * share, :].astype(BF16)
    weight_in[me] = weight_send[me]

    @pl.loop(1, peers)
    def _(p):
        peer = lax.rem(me + p, peers)
        pltpu.make_async_remote_copy(
            src_ref=weight_send.at[peer],
            dst_ref=weight_in.at[me],
            send_sem=weight_send_sem,
            recv_sem=weight_recv_sem,
            device_id=(peer,),
            device_id_type=MESH,
        ).start()

    @pl.loop(0, local_blocks)
    def _(h):
        at = pl.ds(pl.multiple_of(h * LO, LO), LO)
        part[:, at] = part[:, at] + dot(edge[...], count[h], 1, 0)

    pltpu.make_async_copy(returned.at[others], returned.at[others], back_recv_sem).wait()

    @pl.loop(0, nodes // BLOCK)
    def _(step):
        at = pl.ds(pl.multiple_of(step * BLOCK, BLOCK), BLOCK)
        ids = lax.broadcasted_iota(jnp.int32, (remote, BLOCK), 1) + step * BLOCK
        picks = jnp.where(lists_ref[...] == ids, 1.0, 0.0).astype(BF16)
        out_ref[at, :] = (part[:, at] + dot(returned[...], picks, 0, 0)).T

    rest = pl.ds(0, peers - 1)
    pltpu.make_async_copy(weight_in.at[rest], weight_in.at[rest], weight_recv_sem).wait()
    weight_out_ref[...] = jnp.sum(weight_in[...].astype(F32), axis=0)
    pltpu.make_async_copy(packed.at[others], packed.at[others], send_sem).wait()
    pltpu.make_async_copy(send.at[others], send.at[others], back_send_sem).wait()
    pltpu.make_async_copy(weight_send.at[rest], weight_send.at[rest], weight_send_sem).wait()


def body(
    features, self_weight, neighbour_weight, send_lists, hub_nodes, neighbours, counts, cotangent
):
    nodes, width = features.shape
    fan = neighbours.shape[1]
    peers = lax.axis_size("dom")
    per_peer = send_lists.shape[2]
    hubs = hub_nodes.shape[1]
    both = per_peer + hubs
    remote = peers * both
    blocks = (nodes + remote) // LO
    share = 2 * width // peers

    lists = jnp.concatenate(
        [send_lists[0], jnp.broadcast_to(hub_nodes, (peers, hubs))], axis=1
    ).reshape(remote, 1)
    past = neighbours - nodes
    hub_past = past - peers * per_peer
    remapped = jnp.where(
        past < 0,
        neighbours,
        nodes
        + jnp.where(
            hub_past < 0,
            (past // per_peer) * both + past % per_peer,
            (hub_past // hubs) * both + per_peer + hub_past % hubs,
        ),
    )
    usable = jnp.arange(fan, dtype=jnp.int32)[None, :] < counts[:, None]
    index = jnp.where(usable, remapped, -1).reshape(nodes // 16, 16 * fan)
    degree = counts.astype(F32)
    vmem = pl.BlockSpec(memory_space=pltpu.VMEM)
    return pl.pallas_call(
        functools.partial(whole_kernel, peers),
        in_specs=[vmem] * 8,
        out_specs=[vmem] * 3,
        out_shape=[
            jax.ShapeDtypeStruct((nodes, width), BF16),
            jax.ShapeDtypeStruct((nodes, width), F32),
            jax.ShapeDtypeStruct((share, width), F32),
        ],
        scratch_shapes=[
            pltpu.VMEM((remote, width), BF16),
            pltpu.VMEM((remote, width), BF16),
            pltpu.VMEM((blocks, nodes, LO), BF16),
            pltpu.VMEM((nodes, width), F32),
            pltpu.VMEM((width, nodes), BF16),
            pltpu.VMEM((width, nodes), F32),
            pltpu.VMEM((nodes, width), BF16),
            pltpu.VMEM((nodes, width), BF16),
            pltpu.VMEM((remote, width), BF16),
            pltpu.VMEM((remote, width), BF16),
            pltpu.VMEM((2 * width, width), F32),
            pltpu.VMEM((peers, share, width), BF16),
            pltpu.VMEM((peers, share, width), BF16),
        ]
        + [pltpu.SemaphoreType.DMA] * 6,
        compiler_params=pltpu.CompilerParams(
            collective_id=0, has_side_effects=True, vmem_limit_bytes=60 * 1024 * 1024
        ),
        name="whole",
    )(
        index, lists, degree[:, None], degree[None, :], features, cotangent, self_weight,
        neighbour_weight,
    )


def solution(mesh):
    in_specs = (
        P("dom", None),
        P(),
        P(),
        P("dom", None, None),
        P("dom", None),
        P("dom", None),
        P("dom"),
        P("dom", None),
    )
    out_specs = (P("dom", None), P("dom", None), P("dom", None))
    return jax.shard_map(body, mesh=mesh, in_specs=in_specs, out_specs=out_specs, check_vma=False)
```

```python
import functools

import jax
import jax.numpy as jnp
from jax import lax
from jax.experimental import pallas as pl
from jax.experimental.pallas import tpu as pltpu
from jax.sharding import PartitionSpec as P

LO = 256
BLOCK = 256
BF16 = jnp.bfloat16
F32 = jnp.float32
MESH = pl.DeviceIdType.MESH


def dot(a, b, ca, cb):
    return lax.dot_general(a, b, (((ca,), (cb,)), ((), ())), preferred_element_type=F32)


def whole_kernel(
    peers,
    index_ref, lists_ref, hubs_ref, counts_ref, features_ref, cotangent_ref,
    self_ref, neighbour_ref,
    activations_ref, out_ref, weight_out_ref,
    packed, table, count, summed, edge, pre_grad_t, mean_all, send, returned, list_row,
    weight_acc, weight_send, weight_in,
    send_sem, recv_sem, back_send_sem, back_recv_sem, weight_send_sem, weight_recv_sem,
):
    me = lax.axis_index("dom")
    nodes, width = features_ref.shape
    remote = packed.shape[0]
    both = remote // peers
    blocks = count.shape[0]
    local_blocks = nodes // LO
    remote_blocks = blocks - local_blocks
    lanes = index_ref.shape[1]
    fan = lanes // 16
    share = weight_send.shape[1]
    own = pl.ds(pl.multiple_of(me * both, both), both)

    barrier = pltpu.get_barrier_semaphore()

    @pl.loop(1, peers)
    def _(p):
        pl.semaphore_signal(
            barrier, inc=1, device_id=(lax.rem(me + p, peers),), device_id_type=MESH
        )

    per_peer = lists_ref.shape[0]
    hubs = both - per_peer
    spread_hubs = jnp.broadcast_to(hubs_ref[...], (8, hubs))
    for start in range(0, remote, 512):
        row_ids = lax.broadcasted_iota(jnp.int32, (512, peers), 0) + start
        owner = jnp.where(
            row_ids // both == lax.broadcasted_iota(jnp.int32, (512, peers), 1), 1.0, 0.0
        ).astype(BF16)
        slot = lax.broadcasted_iota(jnp.int32, (512, per_peer), 0) % both
        own_slot = slot == lax.broadcasted_iota(jnp.int32, (512, per_peer), 1)
        slot_row = lax.broadcasted_iota(jnp.int32, (per_peer, 512), 1) % both
        own_slot_row = slot_row == lax.broadcasted_iota(jnp.int32, (per_peer, 512), 0)
        hub_slot = lax.broadcasted_iota(jnp.int32, (512, hubs), 0) % both - per_peer
        own_hub = jnp.where(
            hub_slot == lax.broadcasted_iota(jnp.int32, (512, hubs), 1), 1.0, 0.0
        ).astype(BF16)
        column = jnp.zeros((512, 1), F32)
        line = jnp.zeros((1, 512), F32)
        for digit, scale in ((lambda v: v >> 8, 256.0), (lambda v: v & 255, 1.0)):
            sent = digit(lists_ref[...]).astype(F32).astype(BF16)
            hub = digit(spread_hubs).astype(F32).astype(BF16)
            by_row = jnp.where(own_slot, dot(owner, sent, 1, 1), 0.0)
            column = column + scale * (
                jnp.sum(by_row, axis=1, keepdims=True) + dot(own_hub, hub, 1, 1)[:, :1]
            )
            by_column = jnp.where(own_slot_row, dot(sent, owner, 1, 1), 0.0)
            line = line + scale * (
                jnp.sum(by_column, axis=0, keepdims=True) + dot(hub, own_hub, 1, 1)[:1]
            )
        list_row[:, start : start + 512] = jnp.broadcast_to(line, (8, 512)).astype(jnp.int32)
        rows = column.astype(jnp.int32)
        ids = lax.broadcasted_iota(jnp.int32, (512, nodes), 1)
        picks = jnp.where(rows == ids, 1.0, 0.0).astype(BF16)
        packed[start : start + 512, :] = dot(picks, features_ref[...], 1, 0).astype(BF16)
    table[own, :] = packed[own, :]
    pl.semaphore_wait(barrier, peers - 1)

    @pl.loop(1, peers)
    def _(p):
        peer = lax.rem(me + p, peers)
        pltpu.make_async_remote_copy(
            src_ref=packed.at[pl.ds(pl.multiple_of(peer * both, both), both)],
            dst_ref=table.at[own],
            send_sem=send_sem,
            recv_sem=recv_sem,
            device_id=(peer,),
            device_id_type=MESH,
        ).start()

    rows16 = lax.broadcasted_iota(jnp.int32, (16, lanes), 0)
    cols16 = lax.broadcasted_iota(jnp.int32, (16, lanes), 1) // fan
    mine = rows16 == cols16
    low_ids = lax.broadcasted_iota(jnp.int32, (LO, lanes), 0).astype(F32).astype(BF16)
    one = jnp.ones((), BF16)
    zero = jnp.zeros((), BF16)

    @pl.loop(0, nodes // BLOCK)
    def _(step):
        groups = BLOCK // 16
        index = index_ref[pl.ds(pl.multiple_of(step * groups, groups), groups), :]
        highs = (index >> 8).astype(F32)
        lows = (index & (LO - 1)).astype(F32)
        for group in range(groups):
            high = jnp.broadcast_to(highs[group : group + 1, :], (16, lanes)).astype(BF16)
            high = jnp.where(mine, high, -one)
            low = jnp.broadcast_to(lows[group : group + 1, :], (16, lanes)).astype(BF16)
            low = jnp.concatenate([low] * (LO // 16), axis=0)
            low_hot = jnp.where(low_ids == low, one, zero)
            high_hot = jnp.concatenate(
                [jnp.where(high == jnp.full((), h, BF16), one, zero) for h in range(blocks)],
                axis=0,
            )
            counted = dot(high_hot, low_hot, 1, 1).astype(BF16)
            at = pl.ds(pl.multiple_of(step * BLOCK + 16 * group, 16), 16)
            for h in range(blocks):
                count[h, at, :] = counted[16 * h : 16 * h + 16]

    @pl.loop(0, nodes // BLOCK)
    def _(step):
        at = pl.ds(pl.multiple_of(step * BLOCK, BLOCK), BLOCK)
        total = jnp.zeros((BLOCK, width), F32)
        for h in range(local_blocks):
            total = total + dot(count[h, at, :], features_ref[h * LO : (h + 1) * LO, :], 1, 0)
        summed[at, :] = total

    others = pl.ds(0, (peers - 1) * both)
    pltpu.make_async_copy(table.at[others], table.at[others], recv_sem).wait()

    @pl.loop(0, nodes // BLOCK)
    def _(step):
        at = pl.ds(pl.multiple_of(step * BLOCK, BLOCK), BLOCK)
        total = summed[at, :]
        for h in range(remote_blocks):
            total = total + dot(
                count[local_blocks + h, at, :], table[h * LO : (h + 1) * LO, :], 1, 0
            )
        degree = counts_ref[:, at].astype(F32)
        column = jnp.broadcast_to(degree, (128, BLOCK)).T
        mean = (total / jnp.concatenate([column] * (width // 128), axis=1)).astype(BF16)
        mean_all[at, :] = mean
        pre = dot(features_ref[at, :], self_ref[...], 1, 0) + dot(mean, neighbour_ref[...], 1, 0)
        sig = jax.nn.sigmoid(pre)
        activations_ref[at, :] = (pre * sig).astype(BF16)
        grad_pre = (
            cotangent_ref[at, :].astype(F32) * sig * (1.0 + pre * (1.0 - sig))
        ).astype(BF16)
        pre_grad_t[:, at] = grad_pre.T
        edge[:, at] = (dot(neighbour_ref[...], grad_pre, 1, 1) / degree).astype(BF16)
        out_ref[at, :] = dot(grad_pre, self_ref[...], 1, 1)

    for h in range(remote_blocks):
        send[h * LO : (h + 1) * LO, :] = dot(edge[...], count[local_blocks + h], 1, 0).T.astype(BF16)
    returned[own, :] = send[own, :]

    @pl.loop(1, peers)
    def _(p):
        peer = lax.rem(me + p, peers)
        pltpu.make_async_remote_copy(
            src_ref=send.at[pl.ds(pl.multiple_of(peer * both, both), both)],
            dst_ref=returned.at[own],
            send_sem=back_send_sem,
            recv_sem=back_recv_sem,
            device_id=(peer,),
            device_id_type=MESH,
        ).start()

    weight_acc[:width, :] = dot(pre_grad_t[...], features_ref[...], 1, 0).T
    weight_acc[width:, :] = dot(pre_grad_t[...], mean_all[...], 1, 0).T
    for p in range(peers):
        weight_send[p] = weight_acc[p * share : (p + 1) * share, :].astype(BF16)
    weight_in[me] = weight_send[me]

    @pl.loop(1, peers)
    def _(p):
        peer = lax.rem(me + p, peers)
        pltpu.make_async_remote_copy(
            src_ref=weight_send.at[peer],
            dst_ref=weight_in.at[me],
            send_sem=weight_send_sem,
            recv_sem=weight_recv_sem,
            device_id=(peer,),
            device_id_type=MESH,
        ).start()

    @pl.loop(0, local_blocks)
    def _(h):
        at = pl.ds(pl.multiple_of(h * LO, LO), LO)
        out_ref[at, :] = out_ref[at, :] + dot(edge[...], count[h], 1, 0).T

    pltpu.make_async_copy(returned.at[others], returned.at[others], back_recv_sem).wait()

    @pl.loop(0, nodes // BLOCK)
    def _(step):
        at = pl.ds(pl.multiple_of(step * BLOCK, BLOCK), BLOCK)
        ids = lax.broadcasted_iota(jnp.int32, (BLOCK, remote), 0) + step * BLOCK
        picks = jnp.where(list_row[:1, :] == ids, 1.0, 0.0).astype(BF16)
        out_ref[at, :] = out_ref[at, :] + dot(picks, returned[...], 1, 0)

    rest = pl.ds(0, peers - 1)
    pltpu.make_async_copy(weight_in.at[rest], weight_in.at[rest], weight_recv_sem).wait()
    weight_out_ref[...] = jnp.sum(weight_in[...].astype(F32), axis=0)
    pltpu.make_async_copy(packed.at[others], packed.at[others], send_sem).wait()
    pltpu.make_async_copy(send.at[others], send.at[others], back_send_sem).wait()
    pltpu.make_async_copy(weight_send.at[rest], weight_send.at[rest], weight_send_sem).wait()


def body(
    features, self_weight, neighbour_weight, send_lists, hub_nodes, neighbours, counts, cotangent
):
    nodes, width = features.shape
    fan = neighbours.shape[1]
    peers = lax.axis_size("dom")
    per_peer = send_lists.shape[2]
    hubs = hub_nodes.shape[1]
    both = per_peer + hubs
    remote = peers * both
    blocks = (nodes + remote) // LO
    share = 2 * width // peers

    past = neighbours - nodes
    hub_past = past - peers * per_peer
    remapped = jnp.where(
        past < 0,
        neighbours,
        nodes
        + jnp.where(
            hub_past < 0,
            (past // per_peer) * both + past % per_peer,
            (hub_past // hubs) * both + per_peer + hub_past % hubs,
        ),
    )
    usable = jnp.arange(fan, dtype=jnp.int32)[None, :] < counts[:, None]
    index = jnp.where(usable, remapped, -1).reshape(nodes // 16, 16 * fan)
    vmem = pl.BlockSpec(memory_space=pltpu.VMEM)
    return pl.pallas_call(
        functools.partial(whole_kernel, peers),
        in_specs=[vmem] * 8,
        out_specs=[vmem] * 3,
        out_shape=[
            jax.ShapeDtypeStruct((nodes, width), BF16),
            jax.ShapeDtypeStruct((nodes, width), F32),
            jax.ShapeDtypeStruct((share, width), F32),
        ],
        scratch_shapes=[
            pltpu.VMEM((remote, width), BF16),
            pltpu.VMEM((remote, width), BF16),
            pltpu.VMEM((blocks, nodes, LO), BF16),
            pltpu.VMEM((nodes, width), F32),
            pltpu.VMEM((width, nodes), BF16),
            pltpu.VMEM((width, nodes), BF16),
            pltpu.VMEM((nodes, width), BF16),
            pltpu.VMEM((remote, width), BF16),
            pltpu.VMEM((remote, width), BF16),
            pltpu.VMEM((8, remote), jnp.int32),
            pltpu.VMEM((2 * width, width), F32),
            pltpu.VMEM((peers, share, width), BF16),
            pltpu.VMEM((peers, share, width), BF16),
        ]
        + [pltpu.SemaphoreType.DMA] * 6,
        compiler_params=pltpu.CompilerParams(
            collective_id=0, has_side_effects=True, vmem_limit_bytes=60 * 1024 * 1024
        ),
        name="whole",
    )(
        index, send_lists[0].T, hub_nodes, counts[None, :], features, cotangent, self_weight,
        neighbour_weight,
    )


def solution(mesh):
    in_specs = (
        P("dom", None),
        P(),
        P(),
        P("dom", None, None),
        P("dom", None),
        P("dom", None),
        P("dom"),
        P("dom", None),
    )
    out_specs = (P("dom", None), P("dom", None), P("dom", None))
    return jax.shard_map(body, mesh=mesh, in_specs=in_specs, out_specs=out_specs, check_vma=False)
```

```python
import functools

import jax
import jax.numpy as jnp
from jax import lax
from jax.experimental import pallas as pl
from jax.experimental.pallas import tpu as pltpu
from jax.sharding import PartitionSpec as P

LO = 256
BLOCK = 256
BF16 = jnp.bfloat16
F32 = jnp.float32
MESH = pl.DeviceIdType.MESH


def dot(a, b, ca, cb):
    return lax.dot_general(a, b, (((ca,), (cb,)), ((), ())), preferred_element_type=F32)


def quotient(value, size):
    if size & (size - 1) == 0:
        return value >> (size.bit_length() - 1)
    return value // size


def whole_kernel(
    peers,
    index_ref, lists_ref, hubs_ref, counts_ref, features_ref, cotangent_ref,
    self_ref, neighbour_ref,
    activations_out, part_out, returned_out, weight_in_out, list_row_out,
    activations_ref, out_ref, packed, table, count, summed, edge, pre_grad_t, mean_all, send, returned, list_row,
    weight_acc, weight_send, weight_in,
    send_sem, recv_sem, back_send_sem, back_recv_sem, weight_send_sem, weight_recv_sem, out_sem,
):
    me = lax.axis_index("dom")
    nodes, width = features_ref.shape
    remote = packed.shape[0]
    both = remote // peers
    blocks = count.shape[0]
    local_blocks = nodes // LO
    remote_blocks = blocks - local_blocks
    fan = index_ref.shape[0]
    lanes = 16 * fan
    share = weight_send.shape[1]
    own = pl.ds(pl.multiple_of(me * both, both), both)

    barrier = pltpu.get_barrier_semaphore()

    @pl.loop(1, peers)
    def _(p):
        pl.semaphore_signal(
            barrier, inc=1, device_id=(lax.rem(me + p, peers),), device_id_type=MESH
        )

    per_peer = lists_ref.shape[0]
    hubs = both - per_peer
    spread_hubs = jnp.broadcast_to(hubs_ref[...], (8, hubs))
    for start in range(0, remote, 512):
        row_ids = lax.broadcasted_iota(jnp.int32, (512, peers), 0) + start
        owner = jnp.where(
            row_ids // both == lax.broadcasted_iota(jnp.int32, (512, peers), 1), 1.0, 0.0
        ).astype(BF16)
        slot = lax.broadcasted_iota(jnp.int32, (512, per_peer), 0) % both
        own_slot = slot == lax.broadcasted_iota(jnp.int32, (512, per_peer), 1)
        slot_row = lax.broadcasted_iota(jnp.int32, (per_peer, 512), 1) % both
        own_slot_row = slot_row == lax.broadcasted_iota(jnp.int32, (per_peer, 512), 0)
        hub_slot = lax.broadcasted_iota(jnp.int32, (512, hubs), 0) % both - per_peer
        own_hub = jnp.where(
            hub_slot == lax.broadcasted_iota(jnp.int32, (512, hubs), 1), 1.0, 0.0
        ).astype(BF16)
        column = jnp.zeros((512, 1), F32)
        line = jnp.zeros((1, 512), F32)
        for digit, scale in ((lambda v: v >> 8, 256.0), (lambda v: v & 255, 1.0)):
            sent = digit(lists_ref[...]).astype(F32).astype(BF16)
            hub = digit(spread_hubs).astype(F32).astype(BF16)
            by_row = jnp.where(own_slot, dot(owner, sent, 1, 1), 0.0)
            column = column + scale * (
                jnp.sum(by_row, axis=1, keepdims=True) + dot(own_hub, hub, 1, 1)[:, :1]
            )
            by_column = jnp.where(own_slot_row, dot(sent, owner, 1, 1), 0.0)
            line = line + scale * (
                jnp.sum(by_column, axis=0, keepdims=True) + dot(hub, own_hub, 1, 1)[:1]
            )
        list_row[:, start : start + 512] = jnp.broadcast_to(line, (8, 512)).astype(jnp.int32)
        rows = column.astype(jnp.int32)
        ids = lax.broadcasted_iota(jnp.int32, (512, nodes), 1)
        picks = jnp.where(rows == ids, 1.0, 0.0).astype(BF16)
        packed[start : start + 512, :] = dot(picks, features_ref[...], 1, 0).astype(BF16)
    table[own, :] = packed[own, :]
    pl.semaphore_wait(barrier, peers - 1)

    @pl.loop(1, peers)
    def _(p):
        peer = lax.rem(me + p, peers)
        pltpu.make_async_remote_copy(
            src_ref=packed.at[pl.ds(pl.multiple_of(peer * both, both), both)],
            dst_ref=table.at[own],
            send_sem=send_sem,
            recv_sem=recv_sem,
            device_id=(peer,),
            device_id_type=MESH,
        ).start()

    rows16 = lax.broadcasted_iota(jnp.int32, (16, lanes), 0)
    cols16 = lax.broadcasted_iota(jnp.int32, (16, lanes), 1) // fan
    mine = rows16 == cols16
    low_ids = lax.broadcasted_iota(jnp.int32, (LO, lanes), 0).astype(F32).astype(BF16)
    mine_block = (
        lax.broadcasted_iota(jnp.int32, (BLOCK, lanes), 0) & 15
    ) == lax.broadcasted_iota(jnp.int32, (BLOCK, lanes), 1) // fan
    to_lanes = jnp.where(
        lax.broadcasted_iota(jnp.int32, (fan, lanes), 0)
        == lax.broadcasted_iota(jnp.int32, (fan, lanes), 1) % fan,
        1.0,
        0.0,
    ).astype(BF16)
    same_group = jnp.where(
        lax.broadcasted_iota(jnp.int32, (BLOCK, BLOCK), 0) >> 4
        == lax.broadcasted_iota(jnp.int32, (BLOCK, BLOCK), 1) >> 4,
        1.0,
        0.0,
    ).astype(BF16)
    one = jnp.ones((), BF16)
    zero = jnp.zeros((), BF16)

    @pl.loop(0, nodes // BLOCK)
    def _(step):
        groups = BLOCK // 16
        here = pl.ds(pl.multiple_of(step * BLOCK, BLOCK), BLOCK)
        slots = index_ref[:, here]
        past = slots - nodes
        hub_past = past - peers * per_peer
        sent_at = quotient(past, per_peer)
        sent_at = sent_at * both + (past - sent_at * per_peer)
        hub_at = quotient(hub_past, hubs)
        hub_at = hub_at * both + per_peer + (hub_past - hub_at * hubs)
        index = jnp.where(past < 0, slots, nodes + jnp.where(hub_past < 0, sent_at, hub_at))
        used = lax.broadcasted_iota(jnp.int32, (fan, BLOCK), 0) < counts_ref[:, here]
        index = jnp.where(used, index, -1)
        highs = dot((index >> 8).astype(F32).astype(BF16), to_lanes, 0, 0).astype(BF16)
        lows = dot((index & (LO - 1)).astype(F32).astype(BF16), to_lanes, 0, 0)
        lows = jnp.where(mine_block, lows, 0.0).astype(BF16)
        lows = dot(same_group, lows, 1, 0).astype(BF16)
        for group in range(groups):
            high = jnp.where(mine, highs[16 * group : 16 * group + 16], -one)
            low = lows[16 * group : 16 * group + 16]
            low = jnp.concatenate([low] * (LO // 16), axis=0)
            low_hot = jnp.where(low_ids == low, one, zero)
            high_hot = jnp.concatenate(
                [jnp.where(high == jnp.full((), h, BF16), one, zero) for h in range(blocks)],
                axis=0,
            )
            counted = dot(high_hot, low_hot, 1, 1).astype(BF16)
            at = pl.ds(pl.multiple_of(step * BLOCK + 16 * group, 16), 16)
            for h in range(blocks):
                count[h, at, :] = counted[16 * h : 16 * h + 16]

    @pl.loop(0, nodes // BLOCK)
    def _(step):
        at = pl.ds(pl.multiple_of(step * BLOCK, BLOCK), BLOCK)
        total = jnp.zeros((BLOCK, width), F32)
        for h in range(local_blocks):
            total = total + dot(count[h, at, :], features_ref[h * LO : (h + 1) * LO, :], 1, 0)
        summed[at, :] = total

    others = pl.ds(0, (peers - 1) * both)
    pltpu.make_async_copy(table.at[others], table.at[others], recv_sem).wait()

    @pl.loop(0, nodes // BLOCK)
    def _(step):
        at = pl.ds(pl.multiple_of(step * BLOCK, BLOCK), BLOCK)
        total = summed[at, :]
        for h in range(remote_blocks):
            total = total + dot(
                count[local_blocks + h, at, :], table[h * LO : (h + 1) * LO, :], 1, 0
            )
        degree = counts_ref[:, at].astype(F32)
        column = jnp.broadcast_to(degree, (128, BLOCK)).T
        mean = (total / jnp.concatenate([column] * (width // 128), axis=1)).astype(BF16)
        mean_all[at, :] = mean
        pre = dot(features_ref[at, :], self_ref[...], 1, 0) + dot(mean, neighbour_ref[...], 1, 0)
        sig = jax.nn.sigmoid(pre)
        activations_ref[at, :] = (pre * sig).astype(BF16)
        pltpu.make_async_copy(
            activations_ref.at[at], activations_out.at[at], out_sem.at[0]
        ).start()
        grad_pre = (
            cotangent_ref[at, :].astype(F32) * sig * (1.0 + pre * (1.0 - sig))
        ).astype(BF16)
        pre_grad_t[:, at] = grad_pre.T
        edge[:, at] = (dot(neighbour_ref[...], grad_pre, 1, 1) / degree).astype(BF16)
        out_ref[at, :] = dot(grad_pre, self_ref[...], 1, 1)

    for h in range(remote_blocks):
        send[h * LO : (h + 1) * LO, :] = dot(edge[...], count[local_blocks + h], 1, 0).T.astype(BF16)
    returned[own, :] = send[own, :]

    @pl.loop(1, peers)
    def _(p):
        peer = lax.rem(me + p, peers)
        pltpu.make_async_remote_copy(
            src_ref=send.at[pl.ds(pl.multiple_of(peer * both, both), both)],
            dst_ref=returned.at[own],
            send_sem=back_send_sem,
            recv_sem=back_recv_sem,
            device_id=(peer,),
            device_id_type=MESH,
        ).start()

    weight_acc[:width, :] = dot(pre_grad_t[...], features_ref[...], 1, 0).T
    weight_acc[width:, :] = dot(pre_grad_t[...], mean_all[...], 1, 0).T
    for p in range(peers):
        weight_send[p] = weight_acc[p * share : (p + 1) * share, :].astype(BF16)
    weight_in[me] = weight_send[me]

    @pl.loop(1, peers)
    def _(p):
        peer = lax.rem(me + p, peers)
        pltpu.make_async_remote_copy(
            src_ref=weight_send.at[peer],
            dst_ref=weight_in.at[me],
            send_sem=weight_send_sem,
            recv_sem=weight_recv_sem,
            device_id=(peer,),
            device_id_type=MESH,
        ).start()

    @pl.loop(0, local_blocks)
    def _(h):
        at = pl.ds(pl.multiple_of(h * LO, LO), LO)
        out_ref[at, :] = out_ref[at, :] + dot(edge[...], count[h], 1, 0).T
        pltpu.make_async_copy(out_ref.at[at], part_out.at[at], out_sem.at[1]).start()

    pltpu.make_async_copy(returned.at[others], returned.at[others], back_recv_sem).wait()

    back = pltpu.make_async_copy(returned, returned_out, out_sem.at[2])
    back.start()
    rest = pl.ds(0, peers - 1)
    pltpu.make_async_copy(weight_in.at[rest], weight_in.at[rest], weight_recv_sem).wait()
    weights = pltpu.make_async_copy(weight_in, weight_in_out, out_sem.at[3])
    weights.start()
    list_row_out[...] = list_row[...]
    pltpu.make_async_copy(packed.at[others], packed.at[others], send_sem).wait()
    pltpu.make_async_copy(send.at[others], send.at[others], back_send_sem).wait()
    pltpu.make_async_copy(weight_send.at[rest], weight_send.at[rest], weight_send_sem).wait()
    pltpu.make_async_copy(activations_ref, activations_out, out_sem.at[0]).wait()
    pltpu.make_async_copy(out_ref, part_out, out_sem.at[1]).wait()
    back.wait()
    weights.wait()


def final_kernel(
    part_ref, list_ref, returned_ref, weight_in_ref, activations_in,
    out_ref, weight_out_ref, activations_ref,
):
    step = pl.program_id(0)
    rows, remote = out_ref.shape[0], list_ref.shape[1]
    ids = lax.broadcasted_iota(jnp.int32, (rows, remote), 0) + step * rows
    picks = jnp.where(list_ref[:1, :] == ids, 1.0, 0.0).astype(BF16)
    out_ref[...] = part_ref[...] + dot(picks, returned_ref[...], 1, 0)
    activations_ref[...] = activations_in[...]

    @pl.when(step == 0)
    def _():
        weight_out_ref[...] = jnp.sum(weight_in_ref[...].astype(F32), axis=0)


def body(
    features, self_weight, neighbour_weight, send_lists, hub_nodes, neighbours, counts, cotangent
):
    nodes, width = features.shape
    fan = neighbours.shape[1]
    peers = lax.axis_size("dom")
    per_peer = send_lists.shape[2]
    hubs = hub_nodes.shape[1]
    both = per_peer + hubs
    remote = peers * both
    blocks = (nodes + remote) // LO
    share = 2 * width // peers

    vmem = pl.BlockSpec(memory_space=pltpu.VMEM)
    anywhere = pl.BlockSpec(memory_space=pl.ANY)
    activations, part, returned, weight_in, list_row = pl.pallas_call(
        functools.partial(whole_kernel, peers),
        in_specs=[vmem] * 8,
        out_specs=[anywhere] * 4 + [vmem],
        out_shape=[
            jax.ShapeDtypeStruct((nodes, width), BF16),
            jax.ShapeDtypeStruct((nodes, width), F32),
            jax.ShapeDtypeStruct((remote, width), BF16),
            jax.ShapeDtypeStruct((peers, share, width), BF16),
            jax.ShapeDtypeStruct((8, remote), jnp.int32),
        ],
        scratch_shapes=[
            pltpu.VMEM((nodes, width), BF16),
            pltpu.VMEM((nodes, width), F32),
            pltpu.VMEM((remote, width), BF16),
            pltpu.VMEM((remote, width), BF16),
            pltpu.VMEM((blocks, nodes, LO), BF16),
            pltpu.VMEM((nodes, width), F32),
            pltpu.VMEM((width, nodes), BF16),
            pltpu.VMEM((width, nodes), BF16),
            pltpu.VMEM((nodes, width), BF16),
            pltpu.VMEM((remote, width), BF16),
            pltpu.VMEM((remote, width), BF16),
            pltpu.VMEM((8, remote), jnp.int32),
            pltpu.VMEM((2 * width, width), F32),
            pltpu.VMEM((peers, share, width), BF16),
            pltpu.VMEM((peers, share, width), BF16),
        ]
        + [pltpu.SemaphoreType.DMA] * 6
        + [pltpu.SemaphoreType.DMA((4,))],
        compiler_params=pltpu.CompilerParams(
            collective_id=0, has_side_effects=True, vmem_limit_bytes=60 * 1024 * 1024
        ),
        name="whole",
    )(
        neighbours.T, send_lists[0].T, hub_nodes, counts[None, :], features, cotangent,
        self_weight, neighbour_weight,
    )
    rows = 512
    block = pl.BlockSpec((rows, width), lambda i: (i, 0))
    grad_features, grad_weights, activations = pl.pallas_call(
        final_kernel,
        grid=(nodes // rows,),
        in_specs=[
            block,
            pl.BlockSpec((8, remote), lambda i: (0, 0)),
            pl.BlockSpec((remote, width), lambda i: (0, 0)),
            pl.BlockSpec((peers, share, width), lambda i: (0, 0, 0)),
            block,
        ],
        out_specs=[block, pl.BlockSpec((share, width), lambda i: (0, 0)), block],
        out_shape=[
            jax.ShapeDtypeStruct((nodes, width), F32),
            jax.ShapeDtypeStruct((share, width), F32),
            jax.ShapeDtypeStruct((nodes, width), BF16),
        ],
        name="final",
    )(part, list_row, returned, weight_in, activations)
    return (activations, grad_features, grad_weights)


def solution(mesh):
    in_specs = (
        P("dom", None),
        P(),
        P(),
        P("dom", None, None),
        P("dom", None),
        P("dom", None),
        P("dom"),
        P("dom", None),
    )
    out_specs = (P("dom", None), P("dom", None), P("dom", None))
    return jax.shard_map(body, mesh=mesh, in_specs=in_specs, out_specs=out_specs, check_vma=False)
```

```python
import functools

import jax
import jax.numpy as jnp
from jax import lax
from jax.experimental import pallas as pl
from jax.experimental.pallas import tpu as pltpu
from jax.sharding import PartitionSpec as P

LO = 256
BLOCK = 256
BF16 = jnp.bfloat16
F32 = jnp.float32
MESH = pl.DeviceIdType.MESH


def dot(a, b, ca, cb):
    return lax.dot_general(a, b, (((ca,), (cb,)), ((), ())), preferred_element_type=F32)


def whole_kernel(
    peers,
    index_ref, lists_ref, hubs_ref, counts_ref, features_ref, cotangent_ref,
    self_ref, neighbour_ref,
    activations_out, grads_out, weight_out_ref,
    activations_ref, out_ref, packed, table, count, summed, edge, pre_grad_t, mean_all, send, returned, list_row,
    weight_acc, weight_send, weight_in,
    send_sem, recv_sem, back_send_sem, back_recv_sem, weight_send_sem, weight_recv_sem, out_sem,
):
    me = lax.axis_index("dom")
    nodes, width = features_ref.shape
    remote = packed.shape[0]
    both = remote // peers
    blocks = count.shape[0]
    local_blocks = nodes // LO
    remote_blocks = blocks - local_blocks
    lanes = index_ref.shape[1]
    fan = lanes // 16
    share = weight_send.shape[1]
    own = pl.ds(pl.multiple_of(me * both, both), both)

    barrier = pltpu.get_barrier_semaphore()

    @pl.loop(1, peers)
    def _(p):
        pl.semaphore_signal(
            barrier, inc=1, device_id=(lax.rem(me + p, peers),), device_id_type=MESH
        )

    per_peer = lists_ref.shape[0]
    hubs = both - per_peer
    spread_hubs = jnp.broadcast_to(hubs_ref[...], (8, hubs))
    for start in range(0, remote, 512):
        row_ids = lax.broadcasted_iota(jnp.int32, (512, peers), 0) + start
        owner = jnp.where(
            row_ids // both == lax.broadcasted_iota(jnp.int32, (512, peers), 1), 1.0, 0.0
        ).astype(BF16)
        slot = lax.broadcasted_iota(jnp.int32, (512, per_peer), 0) % both
        own_slot = slot == lax.broadcasted_iota(jnp.int32, (512, per_peer), 1)
        slot_row = lax.broadcasted_iota(jnp.int32, (per_peer, 512), 1) % both
        own_slot_row = slot_row == lax.broadcasted_iota(jnp.int32, (per_peer, 512), 0)
        hub_slot = lax.broadcasted_iota(jnp.int32, (512, hubs), 0) % both - per_peer
        own_hub = jnp.where(
            hub_slot == lax.broadcasted_iota(jnp.int32, (512, hubs), 1), 1.0, 0.0
        ).astype(BF16)
        column = jnp.zeros((512, 1), F32)
        line = jnp.zeros((1, 512), F32)
        for digit, scale in ((lambda v: v >> 8, 256.0), (lambda v: v & 255, 1.0)):
            sent = digit(lists_ref[...]).astype(F32).astype(BF16)
            hub = digit(spread_hubs).astype(F32).astype(BF16)
            by_row = jnp.where(own_slot, dot(owner, sent, 1, 1), 0.0)
            column = column + scale * (
                jnp.sum(by_row, axis=1, keepdims=True) + dot(own_hub, hub, 1, 1)[:, :1]
            )
            by_column = jnp.where(own_slot_row, dot(sent, owner, 1, 1), 0.0)
            line = line + scale * (
                jnp.sum(by_column, axis=0, keepdims=True) + dot(hub, own_hub, 1, 1)[:1]
            )
        list_row[:, start : start + 512] = jnp.broadcast_to(line, (8, 512)).astype(jnp.int32)
        rows = column.astype(jnp.int32)
        ids = lax.broadcasted_iota(jnp.int32, (512, nodes), 1)
        picks = jnp.where(rows == ids, 1.0, 0.0).astype(BF16)
        packed[start : start + 512, :] = dot(picks, features_ref[...], 1, 0).astype(BF16)
    table[own, :] = packed[own, :]
    pl.semaphore_wait(barrier, peers - 1)

    @pl.loop(1, peers)
    def _(p):
        peer = lax.rem(me + p, peers)
        pltpu.make_async_remote_copy(
            src_ref=packed.at[pl.ds(pl.multiple_of(peer * both, both), both)],
            dst_ref=table.at[own],
            send_sem=send_sem,
            recv_sem=recv_sem,
            device_id=(peer,),
            device_id_type=MESH,
        ).start()

    rows16 = lax.broadcasted_iota(jnp.int32, (16, lanes), 0)
    cols16 = lax.broadcasted_iota(jnp.int32, (16, lanes), 1) // fan
    mine = rows16 == cols16
    low_ids = lax.broadcasted_iota(jnp.int32, (LO, lanes), 0).astype(F32).astype(BF16)
    one = jnp.ones((), BF16)
    zero = jnp.zeros((), BF16)

    @pl.loop(0, nodes // BLOCK)
    def _(step):
        groups = BLOCK // 16
        index = index_ref[pl.ds(pl.multiple_of(step * groups, groups), groups), :]
        highs = (index >> 8).astype(F32)
        lows = (index & (LO - 1)).astype(F32)
        for group in range(groups):
            high = jnp.broadcast_to(highs[group : group + 1, :], (16, lanes)).astype(BF16)
            high = jnp.where(mine, high, -one)
            low = jnp.broadcast_to(lows[group : group + 1, :], (16, lanes)).astype(BF16)
            low = jnp.concatenate([low] * (LO // 16), axis=0)
            low_hot = jnp.where(low_ids == low, one, zero)
            high_hot = jnp.concatenate(
                [jnp.where(high == jnp.full((), h, BF16), one, zero) for h in range(blocks)],
                axis=0,
            )
            counted = dot(high_hot, low_hot, 1, 1).astype(BF16)
            at = pl.ds(pl.multiple_of(step * BLOCK + 16 * group, 16), 16)
            for h in range(blocks):
                count[h, at, :] = counted[16 * h : 16 * h + 16]

    @pl.loop(0, nodes // BLOCK)
    def _(step):
        at = pl.ds(pl.multiple_of(step * BLOCK, BLOCK), BLOCK)
        total = jnp.zeros((BLOCK, width), F32)
        for h in range(local_blocks):
            total = total + dot(count[h, at, :], features_ref[h * LO : (h + 1) * LO, :], 1, 0)
        summed[at, :] = total

    others = pl.ds(0, (peers - 1) * both)
    pltpu.make_async_copy(table.at[others], table.at[others], recv_sem).wait()

    @pl.loop(0, nodes // BLOCK)
    def _(step):
        at = pl.ds(pl.multiple_of(step * BLOCK, BLOCK), BLOCK)
        total = summed[at, :]
        for h in range(remote_blocks):
            total = total + dot(
                count[local_blocks + h, at, :], table[h * LO : (h + 1) * LO, :], 1, 0
            )
        degree = counts_ref[:, at].astype(F32)
        column = jnp.broadcast_to(degree, (128, BLOCK)).T
        mean = (total / jnp.concatenate([column] * (width // 128), axis=1)).astype(BF16)
        mean_all[at, :] = mean
        pre = dot(features_ref[at, :], self_ref[...], 1, 0) + dot(mean, neighbour_ref[...], 1, 0)
        sig = jax.nn.sigmoid(pre)
        activations_ref[at, :] = (pre * sig).astype(BF16)
        pltpu.make_async_copy(
            activations_ref.at[at], activations_out.at[at], out_sem.at[0]
        ).start()
        grad_pre = (
            cotangent_ref[at, :].astype(F32) * sig * (1.0 + pre * (1.0 - sig))
        ).astype(BF16)
        pre_grad_t[:, at] = grad_pre.T
        edge[:, at] = (dot(neighbour_ref[...], grad_pre, 1, 1) / degree).astype(BF16)
        out_ref[at, :] = dot(grad_pre, self_ref[...], 1, 1)

    for h in range(remote_blocks):
        send[h * LO : (h + 1) * LO, :] = dot(edge[...], count[local_blocks + h], 1, 0).T.astype(BF16)
    returned[own, :] = send[own, :]

    @pl.loop(1, peers)
    def _(p):
        peer = lax.rem(me + p, peers)
        pltpu.make_async_remote_copy(
            src_ref=send.at[pl.ds(pl.multiple_of(peer * both, both), both)],
            dst_ref=returned.at[own],
            send_sem=back_send_sem,
            recv_sem=back_recv_sem,
            device_id=(peer,),
            device_id_type=MESH,
        ).start()

    weight_acc[:width, :] = dot(pre_grad_t[...], features_ref[...], 1, 0).T
    weight_acc[width:, :] = dot(pre_grad_t[...], mean_all[...], 1, 0).T
    for p in range(peers):
        weight_send[p] = weight_acc[p * share : (p + 1) * share, :].astype(BF16)
    weight_in[me] = weight_send[me]

    @pl.loop(1, peers)
    def _(p):
        peer = lax.rem(me + p, peers)
        pltpu.make_async_remote_copy(
            src_ref=weight_send.at[peer],
            dst_ref=weight_in.at[me],
            send_sem=weight_send_sem,
            recv_sem=weight_recv_sem,
            device_id=(peer,),
            device_id_type=MESH,
        ).start()

    @pl.loop(0, local_blocks)
    def _(h):
        at = pl.ds(pl.multiple_of(h * LO, LO), LO)
        out_ref[at, :] = out_ref[at, :] + dot(edge[...], count[h], 1, 0).T

    pltpu.make_async_copy(returned.at[others], returned.at[others], back_recv_sem).wait()

    @pl.loop(0, nodes // BLOCK)
    def _(step):
        at = pl.ds(pl.multiple_of(step * BLOCK, BLOCK), BLOCK)
        ids = lax.broadcasted_iota(jnp.int32, (BLOCK, remote), 0) + step * BLOCK
        picks = jnp.where(list_row[:1, :] == ids, 1.0, 0.0).astype(BF16)
        out_ref[at, :] = out_ref[at, :] + dot(picks, returned[...], 1, 0)
        pltpu.make_async_copy(out_ref.at[at], grads_out.at[at], out_sem.at[1]).start()

    rest = pl.ds(0, peers - 1)
    pltpu.make_async_copy(weight_in.at[rest], weight_in.at[rest], weight_recv_sem).wait()
    weight_out_ref[...] = jnp.sum(weight_in[...].astype(F32), axis=0)
    pltpu.make_async_copy(packed.at[others], packed.at[others], send_sem).wait()
    pltpu.make_async_copy(send.at[others], send.at[others], back_send_sem).wait()
    pltpu.make_async_copy(weight_send.at[rest], weight_send.at[rest], weight_send_sem).wait()
    pltpu.make_async_copy(activations_ref, activations_out, out_sem.at[0]).wait()
    pltpu.make_async_copy(out_ref, grads_out, out_sem.at[1]).wait()


def body(
    features, self_weight, neighbour_weight, send_lists, hub_nodes, neighbours, counts, cotangent
):
    nodes, width = features.shape
    fan = neighbours.shape[1]
    peers = lax.axis_size("dom")
    per_peer = send_lists.shape[2]
    hubs = hub_nodes.shape[1]
    both = per_peer + hubs
    remote = peers * both
    blocks = (nodes + remote) // LO
    share = 2 * width // peers

    past = neighbours - nodes
    hub_past = past - peers * per_peer
    remapped = jnp.where(
        past < 0,
        neighbours,
        nodes
        + jnp.where(
            hub_past < 0,
            (past // per_peer) * both + past % per_peer,
            (hub_past // hubs) * both + per_peer + hub_past % hubs,
        ),
    )
    usable = jnp.arange(fan, dtype=jnp.int32)[None, :] < counts[:, None]
    index = jnp.where(usable, remapped, -1).reshape(nodes // 16, 16 * fan)
    vmem = pl.BlockSpec(memory_space=pltpu.VMEM)
    return pl.pallas_call(
        functools.partial(whole_kernel, peers),
        in_specs=[vmem] * 8,
        out_specs=[pl.BlockSpec(memory_space=pl.ANY)] * 2 + [vmem],
        out_shape=[
            jax.ShapeDtypeStruct((nodes, width), BF16),
            jax.ShapeDtypeStruct((nodes, width), F32),
            jax.ShapeDtypeStruct((share, width), F32),
        ],
        scratch_shapes=[
            pltpu.VMEM((nodes, width), BF16),
            pltpu.VMEM((nodes, width), F32),
            pltpu.VMEM((remote, width), BF16),
            pltpu.VMEM((remote, width), BF16),
            pltpu.VMEM((blocks, nodes, LO), BF16),
            pltpu.VMEM((nodes, width), F32),
            pltpu.VMEM((width, nodes), BF16),
            pltpu.VMEM((width, nodes), BF16),
            pltpu.VMEM((nodes, width), BF16),
            pltpu.VMEM((remote, width), BF16),
            pltpu.VMEM((remote, width), BF16),
            pltpu.VMEM((8, remote), jnp.int32),
            pltpu.VMEM((2 * width, width), F32),
            pltpu.VMEM((peers, share, width), BF16),
            pltpu.VMEM((peers, share, width), BF16),
        ]
        + [pltpu.SemaphoreType.DMA] * 6
        + [pltpu.SemaphoreType.DMA((2,))],
        compiler_params=pltpu.CompilerParams(
            collective_id=0, has_side_effects=True, vmem_limit_bytes=60 * 1024 * 1024
        ),
        name="whole",
    )(
        index, send_lists[0].T, hub_nodes, counts[None, :], features, cotangent, self_weight,
        neighbour_weight,
    )


def solution(mesh):
    in_specs = (
        P("dom", None),
        P(),
        P(),
        P("dom", None, None),
        P("dom", None),
        P("dom", None),
        P("dom"),
        P("dom", None),
    )
    out_specs = (P("dom", None), P("dom", None), P("dom", None))
    return jax.shard_map(body, mesh=mesh, in_specs=in_specs, out_specs=out_specs, check_vma=False)
```
